512 devices in a mesh: ops: 8 (over x, core), sec: 64 (over z, y).
Axes of the slice: x: 4, y: 8, z: 8, core: 2. Of those that a mesh axis runs over, the one named last changes fastest.
Arguments:
- wavefunction: bfloat16 [256, 16, 128, 128], P('sec'), may hold values from -6 to 6
- left_ops: bfloat16 [32, 256, 128, 128], P('ops', 'sec'), may hold values from -0.5 to 0.5
- right_ops: bfloat16 [32, 256, 128, 128], P('ops', 'sec'), may hold values from -0.5 to 0.5
- site_weights: float32 [32, 16], P('ops'), may hold values from -1 to 1
- right_sector: int32 [256, 16], replicated, may hold values from 0 to 255, as said below
- left_dims: int32 [256], replicated, may hold values from 32 to 128
- right_dims: int32 [256], replicated, may hold values from 32 to 128
- basis: bfloat16 [4, 256, 16, 128, 128], P(None, 'sec', None, 'ops')
Outputs:
- sigma: bfloat16 [256, 16, 128, 128], P('sec', None, 'ops')
- correlations: float32 [4], replicated
The draws below stay inside these ranges and needn't reach their ends.
Inputs may be any that keep to these rules, and one draw needn't show every extreme that they name: For each two-site state, right_sector maps the 256 left sectors one to one onto the 256 right sectors. Right sector r lies on index r // 4 of sec and left sector a on index a // 4; the slabs of one index of sec go to every index of sec, 1 slabs to each.
All inputs are finite; a program needn't handle non-finite values.
Results may differ from the reference program's by a relative error of at most 0.0055.
Values may be sent and summed in bfloat16 or wider, within the bound.
A program may use at most 128 MiB of HBM per device.

```python
import math
import jax
import jax.numpy as jnp
from jax import lax

DB = 128
PHYS = 16
SL = 4
NV = 4
NB = 256
TERMS = 32


def draw_right_sector(key, part):
    device_count = NB // SL
    first_key, second_key = jax.random.split(key, 2)
    offsets = jax.random.permutation(first_key, device_count)
    repeat_count = SL * PHYS // device_count
    offset_table = jnp.repeat(offsets, repeat_count)
    offset_table = jax.random.permutation(second_key, offset_table).reshape(SL, PHYS)
    sector_ids = jnp.arange(NB)
    source = sector_ids // SL
    within = sector_ids % SL
    target = (source[:, None] + offset_table[within]) % device_count
    return (target * SL + within[:, None]).astype(jnp.int32)


def draw_basis(key, part):
    shape_full = (NV, NB, PHYS, DB, DB)
    values = jax.random.normal(key, shape_full, jnp.float32)
    block_scale = 0.5 + jnp.arange(NB, dtype=jnp.float32) / NB
    row_scale = 0.5 + jnp.arange(DB, dtype=jnp.float32) / DB
    scaled = values * block_scale[None, :, None, None, None] * row_scale[None, None, None, :, None]
    return (scaled / math.sqrt(NB * PHYS * DB * DB)).astype(jnp.bfloat16)


def touch_ends(values, own_key, smallest, largest):
    shape = values.shape
    place = [jax.random.randint(jax.random.fold_in(own_key, axis), (), 0, shape[axis]) for axis in range(len(shape))]
    values = values.at[tuple(place)].set(smallest)
    longest = shape.index(max(shape))
    place[longest] = (place[longest] + 1) % shape[longest]
    return values.at[tuple(place)].set(largest)


def shard_levels(stream_key, extent, shards, low, high):
    factor_of = 1.0
    for dim, blocks in shards:
        heights = jax.random.uniform(jax.random.fold_in(jax.random.fold_in(stream_key, 6), dim), (blocks,), jnp.float32, low / len(shards), high / len(shards))
        factor_of = factor_of * jnp.repeat(jnp.exp(heights), extent[dim] // blocks).reshape((-1,) + (1,) * (len(extent) - 1 - dim))
    return factor_of


def noise(stream_key, shape, spread, most, cuts=(), held_as=jnp.bfloat16):
    gain = shard_levels(stream_key, shape, cuts, -0.22, 0.18) if cuts else 1.0
    result = jax.random.normal(stream_key, shape, jnp.float32) * spread * gain
    return jnp.minimum(jnp.maximum(result, -most), most).astype(held_as)


def setup_inputs(seed: int = 0) -> dict:
    splits = jax.random.split(jax.random.key(seed), 9)
    wavefunction = noise(splits[0], (NB, PHYS, DB, DB), 1.0, 6.0, ((0, 64),))
    left_ops = noise(splits[1], (TERMS, NB, DB, DB), DB ** -0.5, 0.5, ((0, 8), (1, 64)))
    right_ops = noise(splits[2], (TERMS, NB, DB, DB), DB ** -0.5, 0.5, ((0, 8), (1, 64)))
    site_weights = noise(splits[3], (TERMS, PHYS), TERMS ** -0.5, 1.0, ((0, 8),), jnp.float32)
    right_sector = draw_right_sector(jax.random.fold_in(splits[8], 71), 0)
    left_dims = touch_ends(jax.random.randint(splits[5], (NB,), DB // 4, DB + 1), jax.random.fold_in(splits[5], 1), DB // 4, DB).astype(jnp.int32)
    right_dims = touch_ends(jax.random.randint(splits[6], (NB,), DB // 4, DB + 1), jax.random.fold_in(splits[6], 1), DB // 4, DB).astype(jnp.int32)
    basis = draw_basis(jax.random.fold_in(splits[8], 71), 0)
    return {"wavefunction": wavefunction, "left_ops": left_ops, "right_ops": right_ops, "site_weights": site_weights, "right_sector": right_sector, "left_dims": left_dims, "right_dims": right_dims, "basis": basis}


def reference(wavefunction, left_ops, right_ops, site_weights, right_sector, left_dims, right_dims, basis):
    block_width = wavefunction.shape[-1]
    positions = jnp.arange(block_width)
    dims_right = right_dims[right_sector]
    row_ok = positions[None, :] < left_dims[:, None]
    col_ok = positions[None, None, :] < dims_right[:, :, None]
    keep_mask = row_ok[:, None, :, None] & col_ok[:, :, None, :]
    masked = jnp.where(keep_mask, wavefunction, jnp.zeros_like(wavefunction))

    def one_sector(sector):
        slabs = masked[sector].astype(jnp.float32)
        left_blocks = left_ops[:, sector].astype(jnp.float32)
        products = jnp.einsum("kxy,pyz->kpxz", left_blocks, slabs).astype(jnp.bfloat16)
        right_blocks = right_ops[:, right_sector[sector]].astype(jnp.float32)
        terms_out = jnp.einsum("kpxy,kpyz->kpxz", products.astype(jnp.float32), right_blocks)
        summed = jnp.sum(terms_out * site_weights[:, :, None, None], axis=0)
        return jnp.where(keep_mask[sector], summed, jnp.zeros_like(summed))

    contribution = lax.map(one_sector, jnp.arange(NB))
    inverse = jnp.argsort(right_sector, axis=0)
    sigma = contribution[inverse, jnp.arange(PHYS)[None, :]].astype(jnp.bfloat16)
    sigma_wide = sigma.astype(jnp.float32)

    def project(vector):
        return jnp.sum(vector.astype(jnp.float32) * sigma_wide)

    correlations = lax.map(project, basis)
    return sigma, correlations
```

```python
import jax
import jax.numpy as jnp
from jax import lax
from jax.experimental import pallas as pl
from jax.experimental.pallas import tpu as pltpu
from jax.sharding import Mesh
from jax.sharding import PartitionSpec as P


def contract_kernel(index_ref, weight_ref, slab_ref, left_ref, right_ref, out_ref):
    width = slab_ref.shape[-1]
    terms = left_ref.shape[1]
    peers_y = left_ref.shape[0]
    rows = lax.broadcasted_iota(jnp.int32, (width, width), 0)
    columns = lax.broadcasted_iota(jnp.int32, (width, width), 1)

    def edge(position, carry):
        z_from = position // peers_y
        y_from = position % peers_y
        left_at = index_ref[0, position]
        right_at = index_ref[1, position]
        keep = (rows < index_ref[2, position]) & (columns < index_ref[3, position])
        slab = jnp.where(keep, slab_ref[position].astype(jnp.float32), 0.0).astype(jnp.bfloat16)
        total = jnp.zeros((width, width), jnp.float32)
        for term in range(terms):
            product = jnp.dot(
                left_ref[y_from, term, left_at], slab, preferred_element_type=jnp.float32
            )
            summand = jnp.dot(
                product.astype(jnp.bfloat16),
                right_ref[z_from, term, right_at],
                preferred_element_type=jnp.float32,
            )
            total += summand * weight_ref[term, position]
        out_ref[position] = jnp.where(keep, total, 0.0)
        return carry

    lax.fori_loop(0, slab_ref.shape[0], edge, 0)


def contract(index_table, weight_table, slabs, left_all, right_all):
    smem = pl.BlockSpec(memory_space=pltpu.SMEM)
    vmem = pl.BlockSpec(memory_space=pltpu.VMEM)
    return pl.pallas_call(
        contract_kernel,
        out_shape=jax.ShapeDtypeStruct(slabs.shape, jnp.float32),
        in_specs=[smem, smem, vmem, vmem, vmem],
        out_specs=vmem,
    )(index_table, weight_table, slabs, left_all, right_all)


def per_device(
    wavefunction, left_ops, right_ops, site_weights, right_sector, left_dims, right_dims, basis
):
    sectors, states, width, _ = wavefunction.shape
    terms = left_ops.shape[0]
    size_z, size_y = lax.axis_size("z"), lax.axis_size("y")
    groups = size_z * size_y
    items = sectors * states
    me_z, me_y, me_o = lax.axis_index("z"), lax.axis_index("y"), lax.axis_index("ops")
    right_groups = right_sector.reshape(groups, items)
    row_groups = lax.dynamic_slice_in_dim(right_groups, me_z * size_y, size_y, 0)
    wanted = jnp.arange(size_z, dtype=jnp.int32) * size_y + me_y
    match = (row_groups // sectors)[None, :, :] == wanted[:, None, None]
    item_at = jnp.arange(items, dtype=jnp.int32)
    item = jnp.sum(jnp.where(match, item_at, 0), axis=2)
    right_at = jnp.sum(jnp.where(match, row_groups[None], 0), axis=2)
    source = (me_z * size_y + jnp.arange(size_y, dtype=jnp.int32)) * sectors
    left_at = source[None, :] + item // states
    sector_at = jnp.arange(groups * sectors, dtype=jnp.int32)
    left_dim = jnp.sum(jnp.where(left_at[..., None] == sector_at, left_dims, 0), axis=-1)
    right_dim = jnp.sum(jnp.where(right_at[..., None] == sector_at, right_dims, 0), axis=-1)
    index_table = jnp.stack(
        [
            (item // states).reshape(-1),
            (right_at % sectors).reshape(-1),
            left_dim.reshape(-1),
            right_dim.reshape(-1),
        ]
    )
    state = (item % states).reshape(-1)
    state_at = jnp.arange(states, dtype=jnp.int32)
    weight_table = jnp.sum(
        jnp.where(state[None, :, None] == state_at, site_weights[:, None, :], 0.0), axis=-1
    )
    my_groups = lax.dynamic_index_in_dim(right_groups, me_z * size_y + me_y, 0, keepdims=False)
    targets = me_o * size_y + jnp.arange(size_y, dtype=jnp.int32)
    chosen = jnp.sum(
        jnp.where((my_groups // sectors)[None, :] == targets[:, None], item_at, 0), axis=1
    )
    outgoing = jnp.take(wavefunction.reshape(items, width, width), chosen, axis=0)
    arrived = lax.all_to_all(outgoing, "y", split_axis=0, concat_axis=0, tiled=True)
    slabs = lax.all_gather(arrived, "ops", axis=0, tiled=True)
    left_all = lax.all_gather(left_ops, "y", axis=0)
    right_all = lax.all_gather(right_ops, "z", axis=0)
    partial = contract(index_table, weight_table, slabs, left_all, right_all)
    summed = lax.psum_scatter(partial, "ops", scatter_dimension=1, tiled=True).astype(jnp.bfloat16)
    received = lax.all_to_all(summed, "z", split_axis=0, concat_axis=0, tiled=True)
    owned = (me_z * size_y + me_y) * sectors + jnp.arange(sectors, dtype=jnp.int32)
    slot = jnp.sum(
        jnp.where(right_sector[None] == owned[:, None, None], sector_at[None, :, None] // sectors, 0),
        axis=1,
    )
    sigma = jnp.take(received, slot.reshape(-1), axis=0).reshape(sectors, states, -1, width)
    local = jnp.einsum("vjpxy,jpxy->v", basis, sigma, preferred_element_type=jnp.float32)
    return sigma, lax.psum(local, ("ops", "z", "y"))


def solution(mesh):
    grid = Mesh(mesh.devices.reshape(8, 8, 8), ("ops", "z", "y"))
    sec = ("z", "y")
    in_specs = (
        P(sec, None, None, None),
        P("ops", sec, None, None),
        P("ops", sec, None, None),
        P("ops", None),
        P(),
        P(),
        P(),
        P(None, sec, None, "ops", None),
    )
    out_specs = (P(sec, None, "ops", None), P())
    return jax.shard_map(
        per_device, mesh=grid, in_specs=in_specs, out_specs=out_specs, check_vma=False
    )
```

```python
import jax
import jax.numpy as jnp
from jax import lax
from jax.experimental import pallas as pl
from jax.experimental.pallas import tpu as pltpu
from jax.sharding import Mesh
from jax.sharding import PartitionSpec as P

MESH = pl.DeviceIdType.MESH
RING = 8
CHIPS = 4
DISTANCE = (0, 1, 7, 2, 6, 3, 5, 4)
RANK = tuple(DISTANCE.index(d) for d in range(RING))
READY = (1, 3, 5, 7, 8)


def pair_order():
    order, before = [], 0
    for ready in READY:
        for z_rank in range(ready):
            for y_rank in range(ready):
                if max(z_rank, y_rank) >= before:
                    order.append((z_rank, y_rank))
        before = ready
    return order


ORDER = pair_order()
BOUNDS = (0,) + tuple(ready * ready for ready in READY)


def kernel(
    index_ref,
    weight_ref,
    slot_ref,
    outgoing_ref,
    left_ref,
    right_ref,
    basis_ref,
    sigma_ref,
    sums_ref,
    slab_ref,
    left_land,
    right_land,
    left_all,
    right_all,
    split_ref,
    pair_ref,
    row_ref,
    chip_ref,
    final_ref,
    arrive_ref,
    tally_ref,
    local_sem,
    slab_send,
    slab_recv,
    spread_send,
    spread_recv,
    mate_send,
    mate_recv,
    ring_send,
    ring_recv,
    pair_send,
    pair_recv,
    chip_send,
    chip_recv,
    final_send,
    final_recv,
    tally_send,
    tally_recv,
):
    me_o, me_z, me_y = lax.axis_index("ops"), lax.axis_index("z"), lax.axis_index("y")
    me_x, core = me_o // 2, me_o % 2
    mate = me_x * 2 + 1 - core
    mine = {"ops": me_o, "z": me_z, "y": me_y}
    terms, width = left_ref.shape[0], left_ref.shape[-1]
    half = terms // 2
    started = []

    def device(axis, position):
        return tuple(
            position if name == axis else mine[name] for name in ("ops", "z", "y")
        )

    def send(source, target, send_sem, recv_sem, axis, position):
        copy = pltpu.make_async_remote_copy(
            src_ref=source,
            dst_ref=target,
            send_sem=send_sem,
            recv_sem=recv_sem,
            device_id=device(axis, position),
            device_id_type=MESH,
        )
        copy.start()
        started.append(copy)
        return copy

    def chip_at(step):
        return lax.rem(me_x + step, CHIPS)

    def ring_at(position, step):
        return lax.rem(position + step, RING)

    barrier = pltpu.get_barrier_semaphore()
    for axis in ("ops", "z", "y"):
        for step in range(1, RING):
            pl.semaphore_signal(
                barrier,
                inc=1,
                device_id=device(axis, ring_at(mine[axis], step)),
                device_id_type=MESH,
            )
    pl.semaphore_wait(barrier, 3 * (RING - 1))

    own = pltpu.make_async_copy(
        outgoing_ref.at[me_y], slab_ref.at[me_o, me_y], local_sem
    )
    own.start()
    slab_copies = [
        send(
            outgoing_ref.at[ring_at(me_y, step)],
            slab_ref.at[me_o, me_y],
            slab_send.at[step],
            slab_recv.at[step],
            "y",
            ring_at(me_y, step),
        )
        for step in range(1, RING)
    ]

    sides = ((left_ref, left_land, "y"), (right_ref, right_land, "z"))
    flying = {}

    def pass_on(stage, part):
        for side, (held, land, axis) in enumerate(sides):
            for way in range(2):
                if stage == 3 and part != way:
                    continue
                here = stage if way == 0 else (RING - stage) % RING
                there = stage + 1 if way == 0 else RING - 1 - stage
                terms_at = pl.ds(part * half, half)
                source = held.at[terms_at] if stage == 0 else land.at[RANK[here], terms_at]
                sem = ((side * 2 + way) * 4 + stage) * 2 + part
                flying[side, way, stage, part] = send(
                    source,
                    land.at[RANK[there], terms_at],
                    ring_send.at[sem],
                    ring_recv.at[sem],
                    axis,
                    ring_at(mine[axis], 1 if way == 0 else RING - 1),
                )

    def take_in(stage, part):
        for side in range(2):
            for way in range(2):
                if stage == 3 and part != way:
                    continue
                flying[side, way, stage, part].wait_recv()

    def keep_block(held, kept, rank):
        def one(term, carry):
            kept[rank, term] = held[term]
            return carry

        lax.fori_loop(0, terms, one, 0)

    rows = lax.broadcasted_iota(jnp.int32, (width, width), 0)
    columns = lax.broadcasted_iota(jnp.int32, (width, width), 1)
    share = width // RING

    def contract(stage):
        def one(position, carry):
            slab = slab_ref[index_ref[0, position], index_ref[1, position]]
            z_rank, y_rank = index_ref[2, position], index_ref[3, position]
            left_at, right_at = index_ref[4, position], index_ref[5, position]
            keep = (rows < index_ref[6, position]) & (columns < index_ref[7, position])
            total = jnp.zeros((width, width), jnp.float32)
            for term in range(terms):
                product = jnp.dot(
                    left_all[y_rank, term, left_at], slab, preferred_element_type=jnp.float32
                )
                summand = jnp.dot(
                    product.astype(jnp.bfloat16),
                    right_all[z_rank, term, right_at],
                    preferred_element_type=jnp.float32,
                )
                total += summand * weight_ref[term, position]
            total = jnp.where(keep, total, 0.0)
            for owner in range(RING):
                split_ref[owner % 2, owner // 2, position] = total[
                    owner * share : (owner + 1) * share
                ]
            return carry

        lax.fori_loop(BOUNDS[stage], BOUNDS[stage + 1], one, 0)

    pair_copies, chip_copies = {}, {}

    def span(stage):
        return pl.ds(BOUNDS[stage], BOUNDS[stage + 1] - BOUNDS[stage])

    def to_mate(stage):
        pair_copies[stage] = send(
            split_ref.at[1 - core, :, span(stage)],
            pair_ref.at[:, span(stage)],
            pair_send.at[stage],
            pair_recv.at[stage],
            "ops",
            mate,
        )

    def to_chips(stage):
        pair_copies[stage].wait_recv()

        def one(position, carry):
            for chip in range(CHIPS):
                row_ref[chip, position] = (
                    split_ref[core, chip, position] + pair_ref[chip, position]
                )
            return carry

        lax.fori_loop(BOUNDS[stage], BOUNDS[stage + 1], one, 0)
        for step in range(1, CHIPS):
            chip_copies[stage, step] = send(
                row_ref.at[chip_at(step), span(stage)],
                chip_ref.at[step - 1, span(stage)],
                chip_send.at[stage * CHIPS + step],
                chip_recv.at[stage * CHIPS + step],
                "ops",
                chip_at(step) * 2 + core,
            )

    pass_on(0, 0)
    pass_on(0, 1)
    own.wait()
    for copy in slab_copies:
        copy.wait_recv()
    spread = [
        send(
            slab_ref.at[me_o],
            slab_ref.at[me_o],
            spread_send.at[step],
            spread_recv.at[step],
            "ops",
            chip_at(step) * 2 + core,
        )
        for step in range(1, CHIPS)
    ]
    mates = [
        send(slab_ref.at[me_o], slab_ref.at[me_o], mate_send.at[0], mate_recv.at[0], "ops", mate)
    ]
    keep_block(left_ref, left_all, 0)
    keep_block(right_ref, right_all, 0)
    take_in(0, 0)
    pass_on(1, 0)
    for step in range(1, CHIPS):
        spread[step - 1].wait_recv()
        block = chip_at(CHIPS - step) * 2 + core
        mates.append(
            send(
                slab_ref.at[block],
                slab_ref.at[block],
                mate_send.at[step],
                mate_recv.at[step],
                "ops",
                mate,
            )
        )
    take_in(0, 1)
    pass_on(1, 1)
    for copy in mates:
        copy.wait_recv()

    contract(0)
    to_mate(0)
    for stage in range(1, 5):
        if stage > 1:
            for part in range(2):
                take_in(stage - 1, part)
                if stage < 4:
                    pass_on(stage, part)
        for rank in range(READY[stage - 1], READY[stage]):
            keep_block(left_land.at[rank], left_all, rank)
            keep_block(right_land.at[rank], right_all, rank)
        to_chips(stage - 1)
        contract(stage)
        to_mate(stage)
    to_chips(4)
    for stage in range(5):
        for step in range(1, CHIPS):
            chip_copies[stage, step].wait_recv()

    final_copies = []
    for z_rank in reversed(range(RING)):
        for y_rank in range(RING):
            position = ORDER.index((z_rank, y_rank))
            value = row_ref[me_x, position] + chip_ref[0, position]
            value = value + chip_ref[1, position] + chip_ref[2, position]
            target = final_ref if z_rank else arrive_ref
            target[z_rank, y_rank] = value.astype(jnp.bfloat16)
        if z_rank:
            final_copies.append(
                send(
                    final_ref.at[z_rank],
                    arrive_ref.at[z_rank],
                    final_send.at[z_rank],
                    final_recv.at[z_rank],
                    "z",
                    ring_at(me_z, RING - DISTANCE[z_rank]),
                )
            )
    for copy in final_copies:
        copy.wait_recv()

    vectors = basis_ref.shape[0]

    def project(item, sums):
        value = arrive_ref[slot_ref[0, item], slot_ref[1, item]]
        sigma_ref[item] = value
        wide = value.astype(jnp.float32)
        return tuple(
            sums[vector] + basis_ref[vector, item].astype(jnp.float32) * wide
            for vector in range(vectors)
        )

    zero = jnp.zeros((share, width), jnp.float32)
    sums = lax.fori_loop(0, basis_ref.shape[1], project, (zero,) * vectors)
    now = jnp.concatenate([jnp.sum(value, axis=0, keepdims=True) for value in sums] * 2, axis=0)

    for phase, axis in enumerate(("ops", "z", "y")):
        tally_ref[phase, mine[axis]] = now
        copies = [
            send(
                tally_ref.at[phase, mine[axis]],
                tally_ref.at[phase, mine[axis]],
                tally_send.at[phase * RING + step],
                tally_recv.at[phase * RING + step],
                axis,
                ring_at(mine[axis], step),
            )
            for step in range(1, RING)
        ]
        for copy in copies:
            copy.wait_recv()
        now = tally_ref[phase, 0]
        for other in range(1, RING):
            now = now + tally_ref[phase, other]
    sums_ref[...] = now
    for copy in started:
        copy.wait_send()


def fused(index_table, weight_table, slot_table, outgoing, left_ops, right_ops, basis):
    smem = pl.BlockSpec(memory_space=pltpu.SMEM)
    vmem = pl.BlockSpec(memory_space=pltpu.VMEM)
    terms, sectors, width, _ = left_ops.shape
    pairs = RING * RING
    share = width // RING
    block = (RING, terms, sectors, width, width)
    dma = pltpu.SemaphoreType.DMA
    return pl.pallas_call(
        kernel,
        out_shape=(
            jax.ShapeDtypeStruct((pairs, share, width), jnp.bfloat16),
            jax.ShapeDtypeStruct((2 * basis.shape[0], width), jnp.float32),
        ),
        in_specs=[smem] * 3 + [vmem] * 4,
        out_specs=(vmem, vmem),
        scratch_shapes=[
            pltpu.VMEM((RING, RING, width, width), jnp.bfloat16),
            pltpu.VMEM(block, jnp.bfloat16),
            pltpu.VMEM(block, jnp.bfloat16),
            pltpu.VMEM(block, jnp.bfloat16),
            pltpu.VMEM(block, jnp.bfloat16),
            pltpu.VMEM((2, CHIPS, pairs, share, width), jnp.float32),
            pltpu.VMEM((CHIPS, pairs, share, width), jnp.float32),
            pltpu.VMEM((CHIPS, pairs, share, width), jnp.float32),
            pltpu.VMEM((CHIPS - 1, pairs, share, width), jnp.float32),
            pltpu.VMEM((RING, RING, share, width), jnp.bfloat16),
            pltpu.VMEM((RING, RING, share, width), jnp.bfloat16),
            pltpu.VMEM((3, RING, 2 * basis.shape[0], width), jnp.float32),
            dma,
            dma((RING,)),
            dma((RING,)),
            dma((CHIPS,)),
            dma((CHIPS,)),
            dma((CHIPS,)),
            dma((CHIPS,)),
            dma((32,)),
            dma((32,)),
            dma((5,)),
            dma((5,)),
            dma((5 * CHIPS,)),
            dma((5 * CHIPS,)),
            dma((RING,)),
            dma((RING,)),
            dma((3 * RING,)),
            dma((3 * RING,)),
        ],
        compiler_params=pltpu.CompilerParams(
            collective_id=0, has_side_effects=True, vmem_limit_bytes=48 << 20
        ),
    )(index_table, weight_table, slot_table, outgoing, left_ops, right_ops, basis)


def pick(table, positions):
    places = jnp.arange(table.shape[0], dtype=jnp.int32)
    return jnp.sum(jnp.where(positions[..., None] == places, table, 0), axis=-1)


def per_device(
    wavefunction, left_ops, right_ops, site_weights, right_sector, left_dims, right_dims, basis
):
    sectors, states, width, _ = wavefunction.shape
    groups = RING * RING
    items = sectors * states
    me_z, me_y, me_o = lax.axis_index("z"), lax.axis_index("y"), lax.axis_index("ops")
    right_groups = right_sector.reshape(groups, items)
    item_at = jnp.arange(items, dtype=jnp.int32)
    z_rank = jnp.array([pair[0] for pair in ORDER], jnp.int32)
    y_rank = jnp.array([pair[1] for pair in ORDER], jnp.int32)
    rank = jnp.array(RANK, jnp.int32)
    z_to = (me_z - jnp.array([DISTANCE[pair[0]] for pair in ORDER], jnp.int32)) % RING
    y_from = (me_y - jnp.array([DISTANCE[pair[1]] for pair in ORDER], jnp.int32)) % RING
    row_groups = lax.dynamic_slice_in_dim(right_groups, me_z * RING, RING, 0)
    match_from = y_from[:, None, None] == jnp.arange(RING, dtype=jnp.int32)[None, :, None]
    match = match_from & ((row_groups // sectors)[None] == (z_to * RING + me_y)[:, None, None])
    item = jnp.sum(jnp.where(match, item_at, 0), axis=(1, 2))
    right_at = jnp.sum(jnp.where(match, row_groups[None], 0), axis=(1, 2))
    left_at = (me_z * RING + y_from) * sectors + item // states
    index_table = jnp.stack(
        [
            z_to,
            y_from,
            z_rank,
            y_rank,
            item // states,
            right_at % sectors,
            pick(left_dims, left_at),
            pick(right_dims, right_at),
        ]
    )
    state_at = jnp.arange(states, dtype=jnp.int32)
    weight_table = jnp.sum(
        jnp.where((item % states)[None, :, None] == state_at, site_weights[:, None, :], 0.0), axis=-1
    )
    my_group = me_z * RING + me_y
    my_rights = lax.dynamic_index_in_dim(right_groups, my_group, 0, keepdims=False)
    targets = me_o * RING + jnp.arange(RING, dtype=jnp.int32)
    chosen_match = (my_rights // sectors)[None, :] == targets[:, None]
    chosen = jnp.sum(jnp.where(chosen_match, item_at, 0), axis=1)
    chosen_right = jnp.sum(jnp.where(chosen_match, my_rights[None], 0), axis=1)
    row_end = pick(left_dims, my_group * sectors + chosen // states)
    column_end = pick(right_dims, chosen_right)
    places = jnp.arange(width, dtype=jnp.int32)
    keep = (places[None, :, None] < row_end[:, None, None]) & (
        places[None, None, :] < column_end[:, None, None]
    )
    taken = jnp.take(wavefunction.reshape(items, width, width), chosen, axis=0)
    outgoing = jnp.where(keep, taken, jnp.zeros_like(taken))
    owned = my_group * sectors + jnp.arange(sectors, dtype=jnp.int32)
    sector_at = jnp.arange(groups * sectors, dtype=jnp.int32)
    source = jnp.sum(
        jnp.where(right_sector[None] == owned[:, None, None], sector_at[None, :, None] // sectors, 0),
        axis=1,
    ).reshape(-1)
    slot_table = jnp.stack(
        [pick(rank, (source // RING - me_z) % RING), pick(rank, (me_y - source % RING) % RING)]
    )
    vectors = basis.shape[0]
    sigma, sums = fused(
        index_table,
        weight_table,
        slot_table,
        outgoing,
        left_ops,
        right_ops,
        basis.reshape(vectors, items, -1, width),
    )
    return sigma.reshape(sectors, states, -1, width), jnp.sum(sums[:vectors], axis=1)


def solution(mesh):
    grid = Mesh(mesh.devices.reshape(RING, RING, RING), ("ops", "z", "y"))
    sec = ("z", "y")
    in_specs = (
        P(sec, None, None, None),
        P("ops", sec, None, None),
        P("ops", sec, None, None),
        P("ops", None),
        P(),
        P(),
        P(),
        P(None, sec, None, "ops", None),
    )
    out_specs = (P(sec, None, "ops", None), P())
    return jax.shard_map(
        per_device, mesh=grid, in_specs=in_specs, out_specs=out_specs, check_vma=False
    )
```

```python
import jax
import jax.numpy as jnp
from jax import lax
from jax.experimental import pallas as pl
from jax.experimental.pallas import tpu as pltpu
from jax.sharding import Mesh
from jax.sharding import PartitionSpec as P

MESH = pl.DeviceIdType.MESH
RING = 8
CHIPS = 4
DISTANCE = (0, 1, 7, 2, 6, 3, 5, 4)
RANK = tuple(DISTANCE.index(d) for d in range(RING))
READY = (1, 3, 5, 7, 8)


def pair_order():
    order, before = [], 0
    for ready in READY:
        for z_rank in range(ready):
            for y_rank in range(ready):
                if max(z_rank, y_rank) >= before:
                    order.append((z_rank, y_rank))
        before = ready
    return order


ORDER = pair_order()
CHUNKS = ((1, 0, 9), (2, 9, 25), (3, 25, 33), (3, 33, 41), (3, 41, 49), (4, 49, 57), (4, 57, 64))


def kernel(
    order_ref,
    weight_ref,
    left_dim_ref,
    right_dim_ref,
    sector_ref,
    wave_hbm,
    left_ref,
    right_ref,
    basis_hbm,
    sigma_ref,
    sums_ref,
    wave_ref,
    basis_ref,
    outgoing_ref,
    made_ref,
    table_ref,
    slab_ref,
    left_land,
    right_land,
    left_all,
    right_all,
    split_ref,
    pair_ref,
    row_ref,
    chip_ref,
    final_ref,
    arrive_ref,
    tally_ref,
    local_sem,
    fetch_sem,
    slab_send,
    slab_recv,
    spread_send,
    spread_recv,
    mate_send,
    mate_recv,
    ring_send,
    ring_recv,
    pair_send,
    pair_recv,
    chip_send,
    chip_recv,
    final_send,
    final_recv,
    tally_send,
    tally_recv,
):
    me_o, me_z, me_y = lax.axis_index("ops"), lax.axis_index("z"), lax.axis_index("y")
    me_x, core = me_o // 2, me_o % 2
    mate = me_x * 2 + 1 - core
    mine = {"ops": me_o, "z": me_z, "y": me_y}
    terms, width = left_ref.shape[0], left_ref.shape[-1]
    half = terms // 2
    sectors = left_ref.shape[1]
    states = weight_ref.shape[1]
    my_group = me_z * RING + me_y
    started = []

    def device(axis, position):
        return tuple(
            position if name == axis else mine[name] for name in ("ops", "z", "y")
        )

    def send(source, target, send_sem, recv_sem, axis, position):
        copy = pltpu.make_async_remote_copy(
            src_ref=source,
            dst_ref=target,
            send_sem=send_sem,
            recv_sem=recv_sem,
            device_id=device(axis, position),
            device_id_type=MESH,
        )
        copy.start()
        started.append(copy)
        return copy

    def chip_at(step):
        return lax.rem(me_x + step, CHIPS)

    def ring_at(position, step):
        return lax.rem(position + step, RING)

    fetches = [
        pltpu.make_async_copy(source, target, fetch_sem.at[place])
        for place, (source, target) in enumerate(
            (
                (wave_hbm, wave_ref),
                (left_ref, left_land.at[0]),
                (right_ref, right_land.at[0]),
                (basis_hbm, basis_ref),
            )
        )
    ]
    for fetch in fetches:
        fetch.start()

    barrier = pltpu.get_barrier_semaphore()
    for axis in ("ops", "z", "y"):
        for step in range(1, RING):
            pl.semaphore_signal(
                barrier,
                inc=1,
                device_id=device(axis, ring_at(mine[axis], step)),
                device_id_type=MESH,
            )
    pl.semaphore_wait(barrier, 3 * (RING - 1))

    sides = ((left_ref, left_land, "y"), (right_ref, right_land, "z"))
    flying = {}

    def pass_on(stage, part):
        for side, (held, land, axis) in enumerate(sides):
            for way in range(2):
                if stage == 3 and part != way:
                    continue
                here = stage if way == 0 else (RING - stage) % RING
                there = stage + 1 if way == 0 else RING - 1 - stage
                terms_at = pl.ds(part * half, half)
                source = held.at[terms_at] if stage == 0 else land.at[RANK[here], terms_at]
                sem = ((side * 2 + way) * 4 + stage) * 2 + part
                flying[side, way, stage, part] = send(
                    source,
                    land.at[RANK[there], terms_at],
                    ring_send.at[sem],
                    ring_recv.at[sem],
                    axis,
                    ring_at(mine[axis], 1 if way == 0 else RING - 1),
                )

    def take_in(stage, part):
        for side in range(2):
            for way in range(2):
                if stage == 3 and part != way:
                    continue
                flying[side, way, stage, part].wait_recv()

    def keep_block(held, kept, rank):
        def one(term, carry):
            kept[rank, term] = held[term]
            return carry

        lax.fori_loop(0, terms, one, 0)

    rows = lax.broadcasted_iota(jnp.int32, (width, width), 0)
    columns = lax.broadcasted_iota(jnp.int32, (width, width), 1)
    share = width // RING

    def far(rank):
        return jnp.where(rank % 2 == 1, (rank + 1) // 2, (RING - rank // 2) % RING)

    def make_tables():
        lanes = lax.broadcasted_iota(jnp.int32, (RING, width), 1)
        sublanes = lax.broadcasted_iota(jnp.int32, (RING, 1), 0)
        items = sector_ref.shape[1]
        item_at = lax.broadcasted_iota(jnp.int32, (RING, items), 1)

        def find(group, wanted):
            held = jnp.broadcast_to(sector_ref[pl.ds(group, 1), :], (RING, items))
            match = held // sectors == wanted
            return (
                jnp.max(jnp.where(match, item_at, 0), axis=1, keepdims=True),
                jnp.max(jnp.where(match, held, 0), axis=1, keepdims=True),
            )

        made_ref[...] = jnp.zeros(made_ref.shape, jnp.int32)
        z_to = (me_z + RING - far(sublanes)) % RING
        made = jnp.zeros((RING, width), jnp.int32)
        for y_rank in range(RING):
            group = me_z * RING + ring_at(me_y, RING - DISTANCE[y_rank])
            item, right = find(group, z_to * RING + me_y)
            made = jnp.where(lanes == y_rank, item, made)
            made = jnp.where(lanes == RING + y_rank, right, made)
        item, right = find(my_group, me_o * RING + sublanes)
        made = jnp.where(lanes == 2 * RING, item, made)
        made = jnp.where(lanes == 2 * RING + 1, right, made)
        made_ref[pl.ds(0, RING), :] = made
        table = sector_ref[...]
        group_at = lax.broadcasted_iota(jnp.int32, table.shape, 0)
        for sector in range(sectors):
            match = table == my_group * sectors + sector
            made_ref[pl.ds(RING + sector, 1), pl.ds(0, items)] = jnp.max(
                jnp.where(match, group_at, 0), axis=0, keepdims=True
            )
        copy = pltpu.make_async_copy(made_ref, table_ref, fetch_sem.at[4])
        copy.start()
        copy.wait()

    def kept(left_at, right_at):
        return (rows < left_dim_ref[left_at]) & (columns < right_dim_ref[right_at])

    def pick_slabs():
        def one(place, carry):
            item, right = table_ref[place, 2 * RING], table_ref[place, 2 * RING + 1]
            keep = kept(my_group * sectors + item // states, right)
            slab = jnp.where(keep, wave_ref[item].astype(jnp.float32), 0.0)
            outgoing_ref[place] = slab.astype(jnp.bfloat16)
            return carry

        lax.fori_loop(0, RING, one, 0)

    def contract(chunk):
        def one(position, carry):
            z_rank, y_rank = order_ref[0, position], order_ref[1, position]
            z_to = lax.rem(me_z + RING - order_ref[2, position], RING)
            y_from = lax.rem(me_y + RING - order_ref[3, position], RING)
            item, right = table_ref[z_rank, y_rank], table_ref[z_rank, RING + y_rank]
            left_at, right_at = item // states, right % sectors
            state = item % states
            slab = slab_ref[z_to, y_from]
            keep = kept((me_z * RING + y_from) * sectors + left_at, right)
            total = jnp.zeros((width, width), jnp.float32)
            for term in range(terms):
                product = jnp.dot(
                    left_all[y_rank, term, left_at], slab, preferred_element_type=jnp.float32
                )
                summand = jnp.dot(
                    product.astype(jnp.bfloat16),
                    right_all[z_rank, term, right_at],
                    preferred_element_type=jnp.float32,
                )
                total += summand * weight_ref[term, state]
            total = jnp.where(keep, total, 0.0)
            for owner in range(RING):
                split_ref[owner % 2, owner // 2, position] = total[
                    owner * share : (owner + 1) * share
                ]
            return carry

        lax.fori_loop(CHUNKS[chunk][1], CHUNKS[chunk][2], one, 0)

    pair_copies, chip_copies = {}, {}

    def span(chunk):
        return pl.ds(CHUNKS[chunk][1], CHUNKS[chunk][2] - CHUNKS[chunk][1])

    def to_mate(chunk):
        pair_copies[chunk] = send(
            split_ref.at[1 - core, :, span(chunk)],
            pair_ref.at[:, span(chunk)],
            pair_send.at[chunk],
            pair_recv.at[chunk],
            "ops",
            mate,
        )

    def to_chips(chunk):
        pair_copies[chunk].wait_recv()

        def one(position, carry):
            for chip in range(CHIPS):
                row_ref[chip, position] = (
                    split_ref[core, chip, position] + pair_ref[chip, position]
                )
            return carry

        lax.fori_loop(CHUNKS[chunk][1], CHUNKS[chunk][2], one, 0)
        for step in range(1, CHIPS):
            chip_copies[chunk, step] = send(
                row_ref.at[chip_at(step), span(chunk)],
                chip_ref.at[step - 1, span(chunk)],
                chip_send.at[chunk * CHIPS + step],
                chip_recv.at[chunk * CHIPS + step],
                "ops",
                chip_at(step) * 2 + core,
            )

    pass_on(0, 0)
    pass_on(0, 1)
    make_tables()
    fetches[0].wait()
    pick_slabs()
    own = pltpu.make_async_copy(
        outgoing_ref.at[me_y], slab_ref.at[me_o, me_y], local_sem
    )
    own.start()
    slab_copies = [
        send(
            outgoing_ref.at[ring_at(me_y, step)],
            slab_ref.at[me_o, me_y],
            slab_send.at[step],
            slab_recv.at[step],
            "y",
            ring_at(me_y, step),
        )
        for step in range(1, RING)
    ]

    own.wait()
    for copy in slab_copies:
        copy.wait_recv()
    spread = [
        send(
            slab_ref.at[me_o],
            slab_ref.at[me_o],
            spread_send.at[step],
            spread_recv.at[step],
            "ops",
            chip_at(step) * 2 + core,
        )
        for step in range(1, CHIPS)
    ]
    mates = [
        send(slab_ref.at[me_o], slab_ref.at[me_o], mate_send.at[0], mate_recv.at[0], "ops", mate)
    ]
    fetches[1].wait()
    fetches[2].wait()
    keep_block(left_land.at[0], left_all, 0)
    keep_block(right_land.at[0], right_all, 0)
    take_in(0, 0)
    pass_on(1, 0)
    for step in range(1, CHIPS):
        spread[step - 1].wait_recv()
        block = chip_at(CHIPS - step) * 2 + core
        mates.append(
            send(
                slab_ref.at[block],
                slab_ref.at[block],
                mate_send.at[step],
                mate_recv.at[step],
                "ops",
                mate,
            )
        )
    take_in(0, 1)
    pass_on(1, 1)
    for copy in mates:
        copy.wait_recv()

    stage, waiting = 0, []
    for chunk in range(len(CHUNKS)):
        if CHUNKS[chunk][0] != stage:
            stage = CHUNKS[chunk][0]
            if stage > 1:
                for part in range(2):
                    take_in(stage - 1, part)
                    if stage < 4:
                        pass_on(stage, part)
            for rank in range(READY[stage - 1], READY[stage]):
                keep_block(left_land.at[rank], left_all, rank)
                keep_block(right_land.at[rank], right_all, rank)
            if stage < 4:
                while waiting:
                    to_chips(waiting.pop(0))
        contract(chunk)
        to_mate(chunk)
        while waiting:
            to_chips(waiting.pop(0))
        waiting.append(chunk)
    to_chips(waiting.pop(0))
    for chunk in range(len(CHUNKS)):
        for step in range(1, CHIPS):
            chip_copies[chunk, step].wait_recv()

    final_copies = []
    for z_rank in reversed(range(RING)):
        for y_rank in range(RING):
            position = ORDER.index((z_rank, y_rank))
            value = row_ref[me_x, position] + chip_ref[0, position]
            value = value + chip_ref[1, position] + chip_ref[2, position]
            target = final_ref if z_rank else arrive_ref
            target[z_rank, y_rank] = value.astype(jnp.bfloat16)
        if z_rank:
            final_copies.append(
                send(
                    final_ref.at[z_rank],
                    arrive_ref.at[z_rank],
                    final_send.at[z_rank],
                    final_recv.at[z_rank],
                    "z",
                    ring_at(me_z, RING - DISTANCE[z_rank]),
                )
            )
    for copy in final_copies:
        copy.wait_recv()

    vectors = basis_ref.shape[0]
    fetches[3].wait()

    def near(distance):
        back = jnp.where(distance == 0, 0, 2 * (RING - distance))
        return jnp.where((distance > 0) & (distance <= RING // 2), 2 * distance - 1, back)

    def project(item, sums):
        sector, state = item // states, item % states
        source = table_ref[RING + sector, state]
        for step in range(1, sectors):
            source = jnp.maximum(source, table_ref[RING + sector, step * states + state])
        z_rank = near(lax.rem(source // RING + RING - me_z, RING))
        y_rank = near(lax.rem(me_y + RING - source % RING, RING))
        value = arrive_ref[z_rank, y_rank]
        sigma_ref[item] = value
        wide = value.astype(jnp.float32)
        return tuple(
            sums[vector] + basis_ref[vector, item].astype(jnp.float32) * wide
            for vector in range(vectors)
        )

    zero = jnp.zeros((share, width), jnp.float32)
    sums = lax.fori_loop(0, basis_ref.shape[1], project, (zero,) * vectors)
    now = jnp.concatenate([jnp.sum(value, axis=0, keepdims=True) for value in sums] * 2, axis=0)

    for phase, axis in enumerate(("ops", "z", "y")):
        tally_ref[phase, mine[axis]] = now
        copies = [
            send(
                tally_ref.at[phase, mine[axis]],
                tally_ref.at[phase, mine[axis]],
                tally_send.at[phase * RING + step],
                tally_recv.at[phase * RING + step],
                axis,
                ring_at(mine[axis], step),
            )
            for step in range(1, RING)
        ]
        for copy in copies:
            copy.wait_recv()
        now = tally_ref[phase, 0]
        for other in range(1, RING):
            now = now + tally_ref[phase, other]
    sums_ref[...] = now
    for copy in started:
        copy.wait_send()


def fused(order, site_weights, left_dims, right_dims, sector_table, wave, left_ops, right_ops, basis):
    smem = pl.BlockSpec(memory_space=pltpu.SMEM)
    vmem = pl.BlockSpec(memory_space=pltpu.VMEM)
    hbm = pl.BlockSpec(memory_space=pl.ANY)
    terms, sectors, width, _ = left_ops.shape
    pairs = RING * RING
    share = width // RING
    block = (RING, terms, sectors, width, width)
    dma = pltpu.SemaphoreType.DMA
    bf16, f32, i32 = jnp.bfloat16, jnp.float32, jnp.int32
    chunks = len(CHUNKS)
    return pl.pallas_call(
        kernel,
        out_shape=(
            jax.ShapeDtypeStruct((pairs, share, width), bf16),
            jax.ShapeDtypeStruct((2 * basis.shape[0], width), f32),
        ),
        in_specs=[smem] * 4 + [vmem] + [hbm] * 4,
        out_specs=(vmem, vmem),
        scratch_shapes=[
            pltpu.VMEM(wave.shape, bf16),
            pltpu.VMEM(basis.shape, bf16),
            pltpu.VMEM((RING, width, width), bf16),
            pltpu.VMEM((2 * RING, width), i32),
            pltpu.SMEM((2 * RING, width), i32),
            pltpu.VMEM((RING, RING, width, width), bf16),
            pltpu.VMEM(block, bf16),
            pltpu.VMEM(block, bf16),
            pltpu.VMEM(block, bf16),
            pltpu.VMEM(block, bf16),
            pltpu.VMEM((2, CHIPS, pairs, share, width), f32),
            pltpu.VMEM((CHIPS, pairs, share, width), f32),
            pltpu.VMEM((CHIPS, pairs, share, width), f32),
            pltpu.VMEM((CHIPS - 1, pairs, share, width), f32),
            pltpu.VMEM((RING, RING, share, width), bf16),
            pltpu.VMEM((RING, RING, share, width), bf16),
            pltpu.VMEM((3, RING, 2 * basis.shape[0], width), f32),
            dma,
            dma((5,)),
            dma((RING,)),
            dma((RING,)),
            dma((CHIPS,)),
            dma((CHIPS,)),
            dma((CHIPS,)),
            dma((CHIPS,)),
            dma((32,)),
            dma((32,)),
            dma((chunks,)),
            dma((chunks,)),
            dma((chunks * CHIPS,)),
            dma((chunks * CHIPS,)),
            dma((RING,)),
            dma((RING,)),
            dma((3 * RING,)),
            dma((3 * RING,)),
        ],
        compiler_params=pltpu.CompilerParams(
            collective_id=0, has_side_effects=True, vmem_limit_bytes=52 << 20
        ),
    )(order, site_weights, left_dims, right_dims, sector_table, wave, left_ops, right_ops, basis)


def per_device(
    wavefunction, left_ops, right_ops, site_weights, right_sector, left_dims, right_dims, basis
):
    sectors, states, width, _ = wavefunction.shape
    items = sectors * states
    vectors = basis.shape[0]
    order = jnp.array(
        [
            [pair[0] for pair in ORDER],
            [pair[1] for pair in ORDER],
            [DISTANCE[pair[0]] for pair in ORDER],
            [DISTANCE[pair[1]] for pair in ORDER],
        ],
        jnp.int32,
    )
    sigma, sums = fused(
        order,
        site_weights,
        left_dims,
        right_dims,
        right_sector.reshape(RING * RING, items),
        wavefunction.reshape(items, width, width),
        left_ops,
        right_ops,
        basis.reshape(vectors, items, -1, width),
    )
    return sigma.reshape(sectors, states, -1, width), jnp.sum(sums[:vectors], axis=1)


def solution(mesh):
    grid = Mesh(mesh.devices.reshape(RING, RING, RING), ("ops", "z", "y"))
    sec = ("z", "y")
    in_specs = (
        P(sec, None, None, None),
        P("ops", sec, None, None),
        P("ops", sec, None, None),
        P("ops", None),
        P(),
        P(),
        P(),
        P(None, sec, None, "ops", None),
    )
    out_specs = (P(sec, None, "ops", None), P())
    return jax.shard_map(
        per_device, mesh=grid, in_specs=in_specs, out_specs=out_specs, check_vma=False
    )
```

```python
import jax
import jax.numpy as jnp
from jax import lax
from jax.experimental import pallas as pl
from jax.experimental.pallas import tpu as pltpu
from jax.sharding import Mesh
from jax.sharding import PartitionSpec as P

MESH = pl.DeviceIdType.MESH
RING = 8
CHIPS = 4
DISTANCE = (0, 1, 7, 2, 6, 3, 5, 4)
RANK = tuple(DISTANCE.index(d) for d in range(RING))
READY = (1, 3, 5, 7, 8)


def pair_order():
    order, before = [], 0
    for ready in READY:
        for z_rank in range(ready):
            for y_rank in range(ready):
                if max(z_rank, y_rank) >= before:
                    order.append((z_rank, y_rank))
        before = ready
    return order


ORDER = pair_order()
CHUNKS = ((1, 0, 9), (2, 9, 25), (3, 25, 33), (3, 33, 41), (3, 41, 49), (4, 49, 57), (4, 57, 64))


def kernel(
    order_ref,
    weight_ref,
    left_dim_ref,
    right_dim_ref,
    sector_ref,
    wave_hbm,
    left_ref,
    right_ref,
    basis_hbm,
    sigma_ref,
    sums_ref,
    wave_ref,
    basis_ref,
    outgoing_ref,
    made_ref,
    table_ref,
    slab_ref,
    left_land,
    right_land,
    left_all,
    right_all,
    split_ref,
    pair_ref,
    row_ref,
    relay_ref,
    chip_ref,
    final_ref,
    arrive_ref,
    tally_ref,
    local_sem,
    fetch_sem,
    slab_send,
    slab_recv,
    spread_send,
    spread_recv,
    mate_send,
    mate_recv,
    ring_send,
    ring_recv,
    pair_send,
    pair_recv,
    chip_send,
    chip_recv,
    near_send,
    near_recv,
    final_send,
    final_recv,
    tally_send,
    tally_recv,
):
    me_o, me_z, me_y = lax.axis_index("ops"), lax.axis_index("z"), lax.axis_index("y")
    me_x, core = me_o // 2, me_o % 2
    mate = me_x * 2 + 1 - core
    mine = {"ops": me_o, "z": me_z, "y": me_y}
    terms, width = left_ref.shape[0], left_ref.shape[-1]
    half = terms // 2
    sectors = left_ref.shape[1]
    states = weight_ref.shape[1]
    my_group = me_z * RING + me_y
    started = []

    def device(axis, position):
        return tuple(
            position if name == axis else mine[name] for name in ("ops", "z", "y")
        )

    def send(source, target, send_sem, recv_sem, axis, position):
        copy = pltpu.make_async_remote_copy(
            src_ref=source,
            dst_ref=target,
            send_sem=send_sem,
            recv_sem=recv_sem,
            device_id=device(axis, position),
            device_id_type=MESH,
        )
        copy.start()
        started.append(copy)
        return copy

    def chip_at(step):
        return lax.rem(me_x + step, CHIPS)

    def ring_at(position, step):
        return lax.rem(position + step, RING)

    fetches = [
        pltpu.make_async_copy(source, target, fetch_sem.at[place])
        for place, (source, target) in enumerate(
            (
                (wave_hbm, wave_ref),
                (left_ref, left_land.at[0]),
                (right_ref, right_land.at[0]),
                (basis_hbm, basis_ref),
            )
        )
    ]
    for fetch in fetches:
        fetch.start()

    barrier = pltpu.get_barrier_semaphore()
    for axis in ("ops", "z", "y"):
        for step in range(1, RING):
            pl.semaphore_signal(
                barrier,
                inc=1,
                device_id=device(axis, ring_at(mine[axis], step)),
                device_id_type=MESH,
            )
    pl.semaphore_wait(barrier, 3 * (RING - 1))

    sides = ((left_ref, left_land, "y"), (right_ref, right_land, "z"))
    flying = {}

    def pass_on(stage, part):
        for side, (held, land, axis) in enumerate(sides):
            for way in range(2):
                if stage == 3 and part != way:
                    continue
                here = stage if way == 0 else (RING - stage) % RING
                there = stage + 1 if way == 0 else RING - 1 - stage
                terms_at = pl.ds(part * half, half)
                source = held.at[terms_at] if stage == 0 else land.at[RANK[here], terms_at]
                sem = ((side * 2 + way) * 4 + stage) * 2 + part
                flying[side, way, stage, part] = send(
                    source,
                    land.at[RANK[there], terms_at],
                    ring_send.at[sem],
                    ring_recv.at[sem],
                    axis,
                    ring_at(mine[axis], 1 if way == 0 else RING - 1),
                )

    def take_in(stage, part):
        for side in range(2):
            for way in range(2):
                if stage == 3 and part != way:
                    continue
                flying[side, way, stage, part].wait_recv()

    def keep_block(held, kept, rank):
        def one(term, carry):
            kept[rank, term] = held[term]
            return carry

        lax.fori_loop(0, terms, one, 0)

    rows = lax.broadcasted_iota(jnp.int32, (width, width), 0)
    columns = lax.broadcasted_iota(jnp.int32, (width, width), 1)
    share = width // RING

    def far(rank):
        return jnp.where(rank % 2 == 1, (rank + 1) // 2, (RING - rank // 2) % RING)

    def make_tables():
        lanes = lax.broadcasted_iota(jnp.int32, (RING, width), 1)
        sublanes = lax.broadcasted_iota(jnp.int32, (RING, 1), 0)
        items = sector_ref.shape[1]
        item_at = lax.broadcasted_iota(jnp.int32, (RING, items), 1)

        def find(group, wanted):
            held = jnp.broadcast_to(sector_ref[pl.ds(group, 1), :], (RING, items))
            match = held // sectors == wanted
            return (
                jnp.max(jnp.where(match, item_at, 0), axis=1, keepdims=True),
                jnp.max(jnp.where(match, held, 0), axis=1, keepdims=True),
            )

        made_ref[...] = jnp.zeros(made_ref.shape, jnp.int32)
        z_to = (me_z + RING - far(sublanes)) % RING
        made = jnp.zeros((RING, width), jnp.int32)
        for y_rank in range(RING):
            group = me_z * RING + ring_at(me_y, RING - DISTANCE[y_rank])
            item, right = find(group, z_to * RING + me_y)
            made = jnp.where(lanes == y_rank, item, made)
            made = jnp.where(lanes == RING + y_rank, right, made)
        item, right = find(my_group, me_o * RING + sublanes)
        made = jnp.where(lanes == 2 * RING, item, made)
        made = jnp.where(lanes == 2 * RING + 1, right, made)
        made_ref[pl.ds(0, RING), :] = made
        table = sector_ref[...]
        group_at = lax.broadcasted_iota(jnp.int32, table.shape, 0)
        for sector in range(sectors):
            match = table == my_group * sectors + sector
            made_ref[pl.ds(RING + sector, 1), pl.ds(0, items)] = jnp.max(
                jnp.where(match, group_at, 0), axis=0, keepdims=True
            )
        copy = pltpu.make_async_copy(made_ref, table_ref, fetch_sem.at[4])
        copy.start()
        copy.wait()

    def kept(left_at, right_at):
        return (rows < left_dim_ref[left_at]) & (columns < right_dim_ref[right_at])

    def pick_slabs():
        def one(place, carry):
            item, right = table_ref[place, 2 * RING], table_ref[place, 2 * RING + 1]
            keep = kept(my_group * sectors + item // states, right)
            slab = jnp.where(keep, wave_ref[item].astype(jnp.float32), 0.0)
            outgoing_ref[place] = slab.astype(jnp.bfloat16)
            return carry

        lax.fori_loop(0, RING, one, 0)

    def contract(chunk):
        def one(position, carry):
            z_rank, y_rank = order_ref[0, position], order_ref[1, position]
            z_to = lax.rem(me_z + RING - order_ref[2, position], RING)
            y_from = lax.rem(me_y + RING - order_ref[3, position], RING)
            item, right = table_ref[z_rank, y_rank], table_ref[z_rank, RING + y_rank]
            left_at, right_at = item // states, right % sectors
            state = item % states
            slab = slab_ref[z_to, y_from]
            keep = kept((me_z * RING + y_from) * sectors + left_at, right)
            total = jnp.zeros((width, width), jnp.float32)
            for term in range(terms):
                product = jnp.dot(
                    left_all[y_rank, term, left_at], slab, preferred_element_type=jnp.float32
                )
                summand = jnp.dot(
                    product.astype(jnp.bfloat16),
                    right_all[z_rank, term, right_at],
                    preferred_element_type=jnp.float32,
                )
                total += summand * weight_ref[term, state]
            total = jnp.where(keep, total, 0.0)
            for owner in range(RING):
                split_ref[owner % 2, owner // 2, position] = total[
                    owner * share : (owner + 1) * share
                ]
            return carry

        lax.fori_loop(CHUNKS[chunk][1], CHUNKS[chunk][2], one, 0)

    pair_copies, chip_copies, near_copies = {}, {}, {}

    def part_ends(chunk, way):
        _, first, end = CHUNKS[chunk]
        middle = (first + end) // 2
        return (first, middle) if way == 0 else (middle, end)

    def part_span(chunk, way):
        first, end = part_ends(chunk, way)
        return pl.ds(first, end - first)

    def span(chunk):
        return pl.ds(CHUNKS[chunk][1], CHUNKS[chunk][2] - CHUNKS[chunk][1])

    def to_mate(chunk):
        pair_copies[chunk] = send(
            split_ref.at[1 - core, :, span(chunk)],
            pair_ref.at[:, span(chunk)],
            pair_send.at[chunk],
            pair_recv.at[chunk],
            "ops",
            mate,
        )

    def to_chips(chunk):
        pair_copies[chunk].wait_recv()

        def one(position, carry):
            for chip in range(CHIPS):
                row_ref[chip, position] = (
                    split_ref[core, chip, position] + pair_ref[chip, position]
                )
            return carry

        lax.fori_loop(CHUNKS[chunk][1], CHUNKS[chunk][2], one, 0)
        for way in range(2):
            chip_copies[chunk, way] = send(
                row_ref.at[chip_at(2), part_span(chunk, way)],
                relay_ref.at[part_span(chunk, way)],
                chip_send.at[chunk * 2 + way],
                chip_recv.at[chunk * 2 + way],
                "ops",
                chip_at(1 if way == 0 else CHIPS - 1) * 2 + core,
            )

    def to_near(chunk):
        for way in range(2):
            chip_copies[chunk, way].wait_recv()
            target = chip_at(1 if way == 0 else CHIPS - 1)
            first, end = part_ends(chunk, way)

            def one(position, carry):
                row_ref[target, position] = row_ref[target, position] + relay_ref[position]
                return carry

            lax.fori_loop(first, end, one, 0)
            near_copies[chunk, way] = send(
                row_ref.at[target, span(chunk)],
                chip_ref.at[way, span(chunk)],
                near_send.at[chunk * 2 + way],
                near_recv.at[chunk * 2 + way],
                "ops",
                target * 2 + core,
            )

    pass_on(0, 0)
    make_tables()
    fetches[0].wait()
    pick_slabs()
    own = pltpu.make_async_copy(
        outgoing_ref.at[me_y], slab_ref.at[me_o, me_y], local_sem
    )
    own.start()
    slab_copies = [
        send(
            outgoing_ref.at[ring_at(me_y, step)],
            slab_ref.at[me_o, me_y],
            slab_send.at[step],
            slab_recv.at[step],
            "y",
            ring_at(me_y, step),
        )
        for step in range(1, RING)
    ]

    pass_on(0, 1)
    take_in(0, 0)
    pass_on(1, 0)
    own.wait()
    for copy in slab_copies:
        copy.wait_recv()
    spread = [
        send(
            slab_ref.at[me_o],
            slab_ref.at[me_o],
            spread_send.at[step],
            spread_recv.at[step],
            "ops",
            chip_at(step) * 2 + core,
        )
        for step in range(1, CHIPS)
    ]
    mates = [
        send(slab_ref.at[me_o], slab_ref.at[me_o], mate_send.at[0], mate_recv.at[0], "ops", mate)
    ]
    fetches[1].wait()
    fetches[2].wait()
    keep_block(left_land.at[0], left_all, 0)
    keep_block(right_land.at[0], right_all, 0)
    take_in(0, 1)
    pass_on(1, 1)
    for rank in range(1, READY[1]):
        keep_block(left_land.at[rank], left_all, rank)
        keep_block(right_land.at[rank], right_all, rank)
    for step in range(1, CHIPS):
        spread[step - 1].wait_recv()
        block = chip_at(CHIPS - step) * 2 + core
        mates.append(
            send(
                slab_ref.at[block],
                slab_ref.at[block],
                mate_send.at[step],
                mate_recv.at[step],
                "ops",
                mate,
            )
        )
    take_in(1, 0)
    pass_on(2, 0)
    for copy in mates:
        copy.wait_recv()

    stage, to_split, to_add = 1, [], []
    for chunk in range(len(CHUNKS)):
        if CHUNKS[chunk][0] != stage:
            stage = CHUNKS[chunk][0]
            for part in range(1 if stage == 2 else 0, 2):
                take_in(stage - 1, part)
                if stage < 4:
                    pass_on(stage, part)
            for rank in range(READY[stage - 1], READY[stage]):
                keep_block(left_land.at[rank], left_all, rank)
                keep_block(right_land.at[rank], right_all, rank)
        contract(chunk)
        to_mate(chunk)
        if to_add:
            to_near(to_add.pop(0))
        if to_split:
            to_add.append(to_split.pop(0))
            to_chips(to_add[-1])
        to_split.append(chunk)
    to_add.append(to_split.pop(0))
    to_chips(to_add[-1])
    while to_add:
        to_near(to_add.pop(0))
    for chunk in range(len(CHUNKS)):
        for way in range(2):
            near_copies[chunk, way].wait_recv()

    final_copies = []
    for z_rank in reversed(range(RING)):
        for y_rank in range(RING):
            position = ORDER.index((z_rank, y_rank))
            value = row_ref[me_x, position] + chip_ref[0, position] + chip_ref[1, position]
            target = final_ref if z_rank else arrive_ref
            target[z_rank, y_rank] = value.astype(jnp.bfloat16)
        if z_rank:
            final_copies.append(
                send(
                    final_ref.at[z_rank],
                    arrive_ref.at[z_rank],
                    final_send.at[z_rank],
                    final_recv.at[z_rank],
                    "z",
                    ring_at(me_z, RING - DISTANCE[z_rank]),
                )
            )
    for copy in final_copies:
        copy.wait_recv()

    vectors = basis_ref.shape[0]
    fetches[3].wait()

    def near(distance):
        back = jnp.where(distance == 0, 0, 2 * (RING - distance))
        return jnp.where((distance > 0) & (distance <= RING // 2), 2 * distance - 1, back)

    def project(item, sums):
        sector, state = item // states, item % states
        source = table_ref[RING + sector, state]
        for step in range(1, sectors):
            source = jnp.maximum(source, table_ref[RING + sector, step * states + state])
        z_rank = near(lax.rem(source // RING + RING - me_z, RING))
        y_rank = near(lax.rem(me_y + RING - source % RING, RING))
        value = arrive_ref[z_rank, y_rank]
        sigma_ref[item] = value
        wide = value.astype(jnp.float32)
        return tuple(
            sums[vector] + basis_ref[vector, item].astype(jnp.float32) * wide
            for vector in range(vectors)
        )

    zero = jnp.zeros((share, width), jnp.float32)
    sums = lax.fori_loop(0, basis_ref.shape[1], project, (zero,) * vectors)
    now = jnp.concatenate([jnp.sum(value, axis=0, keepdims=True) for value in sums] * 2, axis=0)

    for phase, axis in enumerate(("ops", "z", "y")):
        tally_ref[phase, mine[axis]] = now
        copies = [
            send(
                tally_ref.at[phase, mine[axis]],
                tally_ref.at[phase, mine[axis]],
                tally_send.at[phase * RING + step],
                tally_recv.at[phase * RING + step],
                axis,
                ring_at(mine[axis], step),
            )
            for step in range(1, RING)
        ]
        for copy in copies:
            copy.wait_recv()
        now = tally_ref[phase, 0]
        for other in range(1, RING):
            now = now + tally_ref[phase, other]
    sums_ref[...] = now
    for copy in started:
        copy.wait_send()


def fused(order, site_weights, left_dims, right_dims, sector_table, wave, left_ops, right_ops, basis):
    smem = pl.BlockSpec(memory_space=pltpu.SMEM)
    vmem = pl.BlockSpec(memory_space=pltpu.VMEM)
    hbm = pl.BlockSpec(memory_space=pl.ANY)
    terms, sectors, width, _ = left_ops.shape
    pairs = RING * RING
    share = width // RING
    block = (RING, terms, sectors, width, width)
    dma = pltpu.SemaphoreType.DMA
    bf16, f32, i32 = jnp.bfloat16, jnp.float32, jnp.int32
    chunks = len(CHUNKS)
    return pl.pallas_call(
        kernel,
        out_shape=(
            jax.ShapeDtypeStruct((pairs, share, width), bf16),
            jax.ShapeDtypeStruct((2 * basis.shape[0], width), f32),
        ),
        in_specs=[smem] * 4 + [vmem] + [hbm] * 4,
        out_specs=(vmem, vmem),
        scratch_shapes=[
            pltpu.VMEM(wave.shape, bf16),
            pltpu.VMEM(basis.shape, bf16),
            pltpu.VMEM((RING, width, width), bf16),
            pltpu.VMEM((2 * RING, width), i32),
            pltpu.SMEM((2 * RING, width), i32),
            pltpu.VMEM((RING, RING, width, width), bf16),
            pltpu.VMEM(block, bf16),
            pltpu.VMEM(block, bf16),
            pltpu.VMEM(block, bf16),
            pltpu.VMEM(block, bf16),
            pltpu.VMEM((2, CHIPS, pairs, share, width), f32),
            pltpu.VMEM((CHIPS, pairs, share, width), f32),
            pltpu.VMEM((CHIPS, pairs, share, width), f32),
            pltpu.VMEM((pairs, share, width), f32),
            pltpu.VMEM((2, pairs, share, width), f32),
            pltpu.VMEM((RING, RING, share, width), bf16),
            pltpu.VMEM((RING, RING, share, width), bf16),
            pltpu.VMEM((3, RING, 2 * basis.shape[0], width), f32),
            dma,
            dma((5,)),
            dma((RING,)),
            dma((RING,)),
            dma((CHIPS,)),
            dma((CHIPS,)),
            dma((CHIPS,)),
            dma((CHIPS,)),
            dma((32,)),
            dma((32,)),
            dma((chunks,)),
            dma((chunks,)),
            dma((chunks * 2,)),
            dma((chunks * 2,)),
            dma((chunks * 2,)),
            dma((chunks * 2,)),
            dma((RING,)),
            dma((RING,)),
            dma((3 * RING,)),
            dma((3 * RING,)),
        ],
        compiler_params=pltpu.CompilerParams(
            collective_id=0, has_side_effects=True, vmem_limit_bytes=67043328
        ),
    )(order, site_weights, left_dims, right_dims, sector_table, wave, left_ops, right_ops, basis)


def per_device(
    wavefunction, left_ops, right_ops, site_weights, right_sector, left_dims, right_dims, basis
):
    sectors, states, width, _ = wavefunction.shape
    items = sectors * states
    vectors = basis.shape[0]
    order = jnp.array(
        [
            [pair[0] for pair in ORDER],
            [pair[1] for pair in ORDER],
            [DISTANCE[pair[0]] for pair in ORDER],
            [DISTANCE[pair[1]] for pair in ORDER],
        ],
        jnp.int32,
    )
    sigma, sums = fused(
        order,
        site_weights,
        left_dims,
        right_dims,
        right_sector.reshape(RING * RING, items),
        wavefunction.reshape(items, width, width),
        left_ops,
        right_ops,
        basis.reshape(vectors, items, -1, width),
    )
    return sigma.reshape(sectors, states, -1, width), jnp.sum(sums[:vectors], axis=1)


def solution(mesh):
    grid = Mesh(mesh.devices.reshape(RING, RING, RING), ("ops", "z", "y"))
    sec = ("z", "y")
    in_specs = (
        P(sec, None, None, None),
        P("ops", sec, None, None),
        P("ops", sec, None, None),
        P("ops", None),
        P(),
        P(),
        P(),
        P(None, sec, None, "ops", None),
    )
    out_specs = (P(sec, None, "ops", None), P())
    return jax.shard_map(
        per_device, mesh=grid, in_specs=in_specs, out_specs=out_specs, check_vma=False
    )
```
